256 devices in a mesh: section: 4 (over z_hi, core), dp: 64 (over z_lo, y, x).
Axes of the slice: x: 4, y: 4, z: 8 (z_hi: 2, z_lo: 4; z = z_hi * 4 + z_lo), core: 2. Of those that a mesh axis runs over, the one named last changes fastest.
Arguments:
- layer_inputs: bfloat16 [4, 64, 512, 4096], P('section', 'dp'), may hold values from -6 to 6
- out_grads: bfloat16 [4, 64, 512, 4096], P('section', 'dp'), may hold values from -6 to 6
- projections: bfloat16 [4, 4096, 128], P('section'), may hold values from -0.09375 to 0.09375
- query_grads: bfloat16 [4, 2048, 4096], P('section', 'dp'), may hold values from -0.59765625 to 0.59765625
- lengths: int32 [64], P('dp'), may hold values from 1 to 512, as said below
Outputs:
- scores: float32 [64, 2048], P('dp', 'section')
The draws below stay inside these ranges and needn't reach their ends.
Inputs may be any that keep to these rules, and one draw needn't show every extreme that they name: `lengths`: some training example fills all 512 slots.
All inputs are finite; a program needn't handle non-finite values.
Results may differ from the reference program's by a relative error of at most 0.005.
Values may be sent and summed in bfloat16 or wider, within the bound.
No kernel may reach another device: no remote copies, remote signals or barrier semaphores. Data moves between devices by JAX's collectives and lax.ppermute only.
A program may use at most 128 MiB of HBM per device.

```python
import jax
import jax.numpy as jnp

D = 4096
RANK = 64
SEQ = 512
LAYERS = 4
EX = 64
QUERIES = 2048


def draw_lengths(key, part):
    drawn = jax.random.randint(jax.random.fold_in(key, 11), (EX,), 1, SEQ + 1)
    full_slot = jax.random.randint(jax.random.fold_in(key, 12), (), 0, EX)
    return jnp.where(jnp.arange(EX) == full_slot, SEQ, drawn).astype(jnp.int32)


def levels(own_key, dims, split, low, top_value):
    gain, own = 1.0, jax.random.fold_in(own_key, 6)
    for dim, shards_of in split:
        steps = jnp.exp(jax.random.uniform(jax.random.fold_in(own, dim), (shards_of,), jnp.float32, low / len(split), top_value / len(split)))
        gain = gain * jnp.repeat(steps, dims[dim] // shards_of).reshape([-1 if axis == dim else 1 for axis in range(len(dims))])
    return gain


def scatter_about(stream_key, shape, width, bound, cuts=(), kind=jnp.bfloat16):
    result = jax.random.normal(stream_key, shape, jnp.float32) * width
    if len(cuts) > 0:
        result = levels(stream_key, shape, cuts, -0.22, 0.18) * result
    return jnp.clip(result, min=-bound, max=bound).astype(kind)


def setup_inputs(seed: int = 0) -> dict:
    seeds = jax.random.split(jax.random.key(seed), 6)
    layer_inputs = scatter_about(seeds[0], (LAYERS, EX, SEQ, D), 1.0, 6.0, ((0, 4), (1, 64)))
    out_grads = scatter_about(seeds[1], (LAYERS, EX, SEQ, D), 1.0, 6.0, ((0, 4), (1, 64)))
    projections = scatter_about(seeds[2], (LAYERS, D, 2 * RANK), D ** -0.5, 0.09375, ((0, 4),))
    query_grads = scatter_about(seeds[3], (LAYERS, QUERIES, RANK * RANK), 0.1, 0.59765625, ((0, 4), (1, 64)))
    lengths = draw_lengths(jax.random.fold_in(seeds[5], 71), 0)
    return {"layer_inputs": layer_inputs, "out_grads": out_grads, "projections": projections, "query_grads": query_grads, "lengths": lengths}


def reference(layer_inputs, out_grads, projections, query_grads, lengths):
    valid_mask = (jnp.arange(SEQ)[None, :] < lengths[:, None]).astype(jnp.float32)
    token_count = lengths.astype(jnp.float32)
    score_total = jnp.zeros((EX, QUERIES), jnp.float32)
    for layer_index in range(LAYERS):
        flat_in = layer_inputs[layer_index].reshape(EX * SEQ, D)
        flat_grad = out_grads[layer_index].reshape(EX * SEQ, D)
        proj_table = projections[layer_index]
        input_side = jnp.dot(flat_in, proj_table[:, :RANK], preferred_element_type=jnp.float32).astype(jnp.bfloat16).reshape(EX, SEQ, RANK)
        grad_side = jnp.dot(flat_grad, proj_table[:, RANK:], preferred_element_type=jnp.float32).astype(jnp.bfloat16).reshape(EX, SEQ, RANK)
        masked = grad_side.astype(jnp.float32) * valid_mask[:, :, None]
        example = jnp.einsum("esa,esb->eab", masked, input_side.astype(jnp.float32)) / token_count[:, None, None]
        example = example.astype(jnp.bfloat16).reshape(EX, RANK * RANK)
        score_total = score_total + jnp.dot(example, query_grads[layer_index].T, preferred_element_type=jnp.float32)
    return score_total
```

```python
import jax
import jax.numpy as jnp
from jax import lax
from jax.sharding import PartitionSpec as P

SIDE = 4
BOTH = ("section", "dp")


def project_layer(inputs, grads, proj_table, valid_mask, token_count):
    low_rank = proj_table.shape[1] // 2
    input_side = jnp.dot(inputs, proj_table[:, :low_rank], preferred_element_type=jnp.float32)
    grad_side = jnp.dot(grads, proj_table[:, low_rank:], preferred_element_type=jnp.float32)
    masked = grad_side.astype(jnp.bfloat16) * valid_mask[:, None]
    summed = (
        jnp.einsum(
            "sa,sb->ab", masked, input_side.astype(jnp.bfloat16), preferred_element_type=jnp.float32
        )
        / token_count
    )
    return summed.astype(jnp.bfloat16).reshape(1, 1, low_rank * low_rank)


def on_device(n_sections, n_dp, layer_inputs, out_grads, projections, query_grads, lengths):
    seq_len = layer_inputs.shape[2]
    n_lines = n_dp // SIDE
    index = lax.axis_index("dp")
    x_pos, z_pos = index % SIDE, index // (SIDE * SIDE)
    my_section = lax.axis_index("section")

    own = query_grads[0]
    blocks = [own]
    for k in range(1, SIDE):
        pairs = []
        for s in range(n_sections):
            for line in range(n_lines):
                base = s * n_dp + line * SIDE
                pairs += [(base + x, base + (x - k) % SIDE) for x in range(SIDE)]
        blocks.append(lax.ppermute(own, BOTH, pairs))

    valid_mask = (lax.iota(jnp.int32, seq_len) < lengths[0]).astype(jnp.bfloat16)
    example = project_layer(
        layer_inputs[0, 0], out_grads[0, 0], projections[0], valid_mask, lengths[0].astype(jnp.float32)
    )

    plane = [[line * SIDE + x for line in range(n_lines)] for x in range(SIDE)]
    examples = lax.all_to_all(
        jnp.broadcast_to(example, (n_lines,) + example.shape[1:]),
        "dp",
        0,
        0,
        tiled=True,
        axis_index_groups=plane,
    )[:, 0]

    parts = [
        lax.dot_general(examples, b, (((1,), (1,)), ((), ())), preferred_element_type=jnp.float32)
        for b in blocks
    ]
    width = own.shape[0]
    twice = jnp.concatenate(parts + parts, axis=1)
    scores = lax.dynamic_slice(
        twice, (0, ((SIDE - x_pos) % SIDE) * width), (n_lines, SIDE * width)
    )

    keep = (jnp.arange(n_sections) == z_pos)[:, None, None]
    send = jnp.where(keep, scores[None], 0.0).reshape(n_sections * n_lines, 1, SIDE * width)
    over = [
        [s * n_dp + line * SIDE + x for s in range(n_sections) for line in range(n_lines)]
        for x in range(SIDE)
    ]
    got = lax.all_to_all(send, BOTH, 0, 0, tiled=True, axis_index_groups=over)
    got = got.reshape(n_sections, n_sections, SIDE, SIDE * width)
    return got.sum((0, 1)).reshape(1, SIDE * SIDE * width)


def solution(mesh):
    placed = (
        P("section", "dp", None, None),
        P("section", "dp", None, None),
        P("section", None, None),
        P("section", "dp", None),
        P("dp"),
    )

    def body(*args):
        return on_device(mesh.shape["section"], mesh.shape["dp"], *args)

    return jax.shard_map(
        body, mesh=mesh, in_specs=placed, out_specs=P("dp", "section"), check_vma=False
    )
```

```python
import functools

import jax
import jax.numpy as jnp
from jax import lax
from jax.experimental import pallas as pl
from jax.experimental.pallas import tpu as pltpu
from jax.sharding import PartitionSpec as P

SIDE = 4
BOTH = ("section", "dp")
LANES = 128
CHUNKS = 4


def example_kernel(
    len_ref, in_hbm, grad_hbm, proj_hbm, out_ref, in_buf, grad_buf, proj_buf, staged, in_sem, grad_sem, proj_sem
):
    width = proj_buf.shape[0] // CHUNKS
    rank = proj_buf.shape[1] // 2
    copies = []
    for c in range(CHUNKS):
        cols = pl.ds(c * width, width)
        trio = (
            pltpu.make_async_copy(proj_hbm.at[0, cols, :], proj_buf.at[cols, :], proj_sem.at[c]),
            pltpu.make_async_copy(in_hbm.at[0, 0, :, cols], in_buf.at[:, cols], in_sem.at[c]),
            pltpu.make_async_copy(grad_hbm.at[0, 0, :, cols], grad_buf.at[:, cols], grad_sem.at[c]),
        )
        for copy in trio:
            copy.start()
        copies.append(trio)
    input_side = grad_side = None
    for c in range(CHUNKS):
        cols = slice(c * width, (c + 1) * width)
        for copy in copies[c]:
            copy.wait()
        table = proj_buf[cols, :]
        a = jnp.dot(in_buf[:, cols], table, preferred_element_type=jnp.float32)
        b = jnp.dot(grad_buf[:, cols], table, preferred_element_type=jnp.float32)
        input_side = a if input_side is None else input_side + a
        grad_side = b if grad_side is None else grad_side + b
    input_side = input_side[:, :rank].astype(jnp.bfloat16)
    grad_side = grad_side[:, rank:].astype(jnp.bfloat16)
    count = len_ref[0]
    real = lax.broadcasted_iota(jnp.int32, grad_side.shape, 0) < count
    grad_side = jnp.where(real, grad_side, jnp.zeros_like(grad_side))
    summed = lax.dot_general(
        grad_side, input_side, (((0,), (0,)), ((), ())), preferred_element_type=jnp.float32
    )
    staged[...] = summed / count.astype(jnp.float32)
    half = rank // 2
    flat = jnp.concatenate(
        [staged[pl.ds(0, half, stride=2), :], staged[pl.ds(1, half, stride=2), :]], axis=1
    ).astype(jnp.bfloat16)
    for i in range(out_ref.shape[0]):
        out_ref[i] = flat


def example_copies(n_copies, lengths, layer_inputs, out_grads, projections):
    tokens, model = layer_inputs.shape[2:]
    both = projections.shape[2]
    rank = both // 2
    hbm = pl.BlockSpec(memory_space=pltpu.HBM)
    return pl.pallas_call(
        example_kernel,
        out_shape=jax.ShapeDtypeStruct((n_copies, rank * rank // LANES, LANES), jnp.bfloat16),
        in_specs=[pl.BlockSpec(memory_space=pltpu.SMEM), hbm, hbm, hbm],
        out_specs=pl.BlockSpec(memory_space=pltpu.VMEM),
        scratch_shapes=[
            pltpu.VMEM((tokens, model), jnp.bfloat16),
            pltpu.VMEM((tokens, model), jnp.bfloat16),
            pltpu.VMEM((model, both), jnp.bfloat16),
            pltpu.VMEM((rank, rank), jnp.float32),
            pltpu.SemaphoreType.DMA((CHUNKS,)),
            pltpu.SemaphoreType.DMA((CHUNKS,)),
            pltpu.SemaphoreType.DMA((CHUNKS,)),
        ],
        compiler_params=pltpu.CompilerParams(vmem_limit_bytes=56 << 20),
        cost_estimate=pl.CostEstimate(
            flops=COST_FLOPS, bytes_accessed=9 << 20, transcendentals=0
        ),
        name="example_gradient",
    )(lengths, layer_inputs, out_grads, projections)


COST_FLOPS = 1 << 31


def score_kernel(n_sections, got_ref, *rest):
    block_refs, (out_ref, wide) = rest[:SIDE], rest[SIDE:]
    index = lax.axis_index("dp")
    x_pos, z_pos = lax.rem(index, SIDE), lax.div(index, SIDE * SIDE)
    n, rows, lanes = got_ref.shape
    wide[...] = got_ref[...].reshape(n * rows, lanes).astype(jnp.float32)
    examples = jnp.concatenate(
        [wide[pl.ds(c, n, stride=rows), :] for c in range(rows)], axis=1
    ).astype(jnp.bfloat16)
    queries = jnp.concatenate([b[...] for b in block_refs], axis=0)
    scores = lax.dot_general(
        examples, queries, (((1,), (1,)), ((), ())), preferred_element_type=jnp.float32
    )
    scores = pltpu.roll(scores, x_pos * (scores.shape[1] // SIDE), 1)
    for s in range(n_sections):
        out_ref[s * n : (s + 1) * n, :] = jnp.where(z_pos == s, scores, jnp.zeros_like(scores))


def score_rows(n_sections, examples, blocks):
    n, rows, lanes = examples.shape
    vmem = pl.BlockSpec(memory_space=pltpu.VMEM)
    return pl.pallas_call(
        functools.partial(score_kernel, n_sections),
        out_shape=jax.ShapeDtypeStruct((n_sections * n, SIDE * blocks[0].shape[0]), jnp.float32),
        in_specs=[vmem] * (1 + SIDE),
        out_specs=vmem,
        scratch_shapes=[pltpu.VMEM((n * rows, lanes), jnp.float32)],
        compiler_params=pltpu.CompilerParams(vmem_limit_bytes=8 << 20),
        name="scores",
    )(examples, *blocks)


def on_device(n_sections, n_dp, layer_inputs, out_grads, projections, query_grads, lengths):
    n_lines = n_dp // SIDE

    own = query_grads[0]
    blocks = [own]
    for k in range(1, SIDE):
        pairs = []
        for s in range(n_sections):
            for line in range(n_lines):
                base = s * n_dp + line * SIDE
                pairs += [(base + x, base + (x - k) % SIDE) for x in range(SIDE)]
        blocks.append(lax.ppermute(own, BOTH, pairs))

    plane = [[line * SIDE + x for line in range(n_lines)] for x in range(SIDE)]
    copies = example_copies(n_lines, lengths, layer_inputs, out_grads, projections)
    examples = lax.all_to_all(copies, "dp", 0, 0, tiled=True, axis_index_groups=plane)

    send = score_rows(n_sections, examples, blocks)
    over = [
        [s * n_dp + line * SIDE + x for s in range(n_sections) for line in range(n_lines)]
        for x in range(SIDE)
    ]
    got = lax.all_to_all(send[:, None], BOTH, 0, 0, tiled=True, axis_index_groups=over)
    got = got.reshape(n_sections, n_sections, SIDE, send.shape[1])
    return got.sum((0, 1)).reshape(1, SIDE * send.shape[1])


def solution(mesh):
    placed = (
        P("section", "dp", None, None),
        P("section", "dp", None, None),
        P("section", None, None),
        P("section", "dp", None),
        P("dp"),
    )

    def body(*args):
        return on_device(mesh.shape["section"], mesh.shape["dp"], *args)

    return jax.shard_map(
        body, mesh=mesh, in_specs=placed, out_specs=P("dp", "section"), check_vma=False
    )
```

```python
import functools

import jax
import jax.numpy as jnp
from jax import lax
from jax.experimental import pallas as pl
from jax.experimental.pallas import tpu as pltpu
from jax.sharding import PartitionSpec as P

SIDE = 4
BOTH = ("section", "dp")
LANES = 128


def example_kernel(len_ref, in_ref, grad_ref, proj_ref, out_ref, staged):
    rank = proj_ref.shape[2] // 2
    table = proj_ref[0]
    input_side = jnp.dot(in_ref[0, 0], table, preferred_element_type=jnp.float32)
    grad_side = jnp.dot(grad_ref[0, 0], table, preferred_element_type=jnp.float32)
    input_side = input_side[:, :rank].astype(jnp.bfloat16)
    grad_side = grad_side[:, rank:].astype(jnp.bfloat16)
    count = len_ref[0]
    real = lax.broadcasted_iota(jnp.int32, grad_side.shape, 0) < count
    grad_side = jnp.where(real, grad_side, jnp.zeros_like(grad_side))
    summed = lax.dot_general(
        grad_side, input_side, (((0,), (0,)), ((), ())), preferred_element_type=jnp.float32
    )
    staged[...] = summed / count.astype(jnp.float32)
    half = rank // 2
    flat = jnp.concatenate(
        [staged[pl.ds(0, half, stride=2), :], staged[pl.ds(1, half, stride=2), :]], axis=1
    ).astype(jnp.bfloat16)
    for i in range(out_ref.shape[0]):
        out_ref[i] = flat


def example_copies(n_copies, lengths, layer_inputs, out_grads, projections):
    both = projections.shape[2]
    rank = both // 2
    vmem = pl.BlockSpec(memory_space=pltpu.VMEM)
    return pl.pallas_call(
        example_kernel,
        out_shape=jax.ShapeDtypeStruct((n_copies, rank * rank // LANES, LANES), jnp.bfloat16),
        in_specs=[pl.BlockSpec(memory_space=pltpu.SMEM), vmem, vmem, vmem],
        out_specs=vmem,
        scratch_shapes=[pltpu.VMEM((rank, rank), jnp.float32)],
        compiler_params=pltpu.CompilerParams(vmem_limit_bytes=16 << 20),
        cost_estimate=pl.CostEstimate(
            flops=COST_FLOPS, bytes_accessed=9 << 20, transcendentals=0
        ),
        name="example_gradient",
    )(lengths, layer_inputs, out_grads, projections)


COST_FLOPS = 1 << 31


def score_kernel(n_sections, got_ref, *rest):
    block_refs, (out_ref, wide) = rest[:SIDE], rest[SIDE:]
    index = lax.axis_index("dp")
    x_pos, z_pos = lax.rem(index, SIDE), lax.div(index, SIDE * SIDE)
    n, rows, lanes = got_ref.shape
    wide[...] = got_ref[...].reshape(n * rows, lanes).astype(jnp.float32)
    examples = jnp.concatenate(
        [wide[pl.ds(c, n, stride=rows), :] for c in range(rows)], axis=1
    ).astype(jnp.bfloat16)
    queries = jnp.concatenate([b[...] for b in block_refs], axis=0)
    scores = lax.dot_general(
        examples, queries, (((1,), (1,)), ((), ())), preferred_element_type=jnp.float32
    )
    width = scores.shape[1] // SIDE
    scores = pltpu.roll(scores, lax.div(x_pos, 2) * (2 * width), 1)
    lane = lax.broadcasted_iota(jnp.int32, scores.shape, 1)
    paired = jnp.where(
        lax.rem(lax.div(lane, width), 2) == 0,
        pltpu.roll(scores, (SIDE - 1) * width, 1),
        pltpu.roll(scores, width, 1),
    )
    scores = jnp.where(lax.rem(x_pos, 2) == 1, paired, scores)
    for s in range(n_sections):
        row = (n_sections - 1 - s) * n
        out_ref[row : row + n, :] = jnp.where(z_pos == s, scores, jnp.zeros_like(scores))


def score_rows(n_sections, examples, blocks):
    n, rows, lanes = examples.shape
    vmem = pl.BlockSpec(memory_space=pltpu.VMEM)
    return pl.pallas_call(
        functools.partial(score_kernel, n_sections),
        out_shape=jax.ShapeDtypeStruct((n_sections * n, SIDE * blocks[0].shape[0]), jnp.float32),
        in_specs=[vmem] * (1 + SIDE),
        out_specs=vmem,
        scratch_shapes=[pltpu.VMEM((n * rows, lanes), jnp.float32)],
        compiler_params=pltpu.CompilerParams(vmem_limit_bytes=8 << 20),
        name="scores",
    )(examples, *blocks)


def total_kernel(got_ref, out_ref):
    n, lanes = got_ref.shape
    both = got_ref[0 : 2 * SIDE, :]
    for r in range(2 * SIDE, n, 2 * SIDE):
        both = both + got_ref[r : r + 2 * SIDE, :]
    for y in range(SIDE):
        r = SIDE - 1 - y
        out_ref[:, y * lanes : (y + 1) * lanes] = both[r : r + 1] + both[r + SIDE : r + SIDE + 1]


def total(got):
    vmem = pl.BlockSpec(memory_space=pltpu.VMEM)
    return pl.pallas_call(
        total_kernel,
        out_shape=jax.ShapeDtypeStruct((1, SIDE * got.shape[1]), jnp.float32),
        in_specs=[vmem],
        out_specs=vmem,
        compiler_params=pltpu.CompilerParams(vmem_limit_bytes=4 << 20),
        name="total",
    )(got)


def keep_kernel(in_ref, out_ref):
    out_ref[...] = in_ref[0]


def kept(block):
    vmem = pl.BlockSpec(memory_space=pltpu.VMEM)
    return pl.pallas_call(
        keep_kernel,
        out_shape=jax.ShapeDtypeStruct(block.shape[1:], block.dtype),
        in_specs=[vmem],
        out_specs=vmem,
        compiler_params=pltpu.CompilerParams(vmem_limit_bytes=4 << 20),
        cost_estimate=pl.CostEstimate(flops=COST_FLOPS * 8, bytes_accessed=9 << 20, transcendentals=0),
        name="own_queries",
    )(block)


def on_device(n_sections, n_dp, layer_inputs, out_grads, projections, query_grads, lengths):
    n_lines = n_dp // SIDE

    own = kept(query_grads)
    blocks = [own]
    for k in range(1, SIDE):
        pairs = []
        for s in range(n_sections):
            for line in range(n_lines):
                base = s * n_dp + line * SIDE
                pairs += [(base + x, base + (x ^ k)) for x in range(SIDE)]
        blocks.append(lax.ppermute(own, BOTH, pairs))

    lines = list(range(n_lines))[::-1]
    sections = list(range(n_sections))[::-1]

    plane = [[line * SIDE + x for line in lines] for x in range(SIDE)]
    copies = example_copies(n_lines, lengths, layer_inputs, out_grads, projections)
    examples = lax.all_to_all(copies, "dp", 0, 0, tiled=True, axis_index_groups=plane)

    send = score_rows(n_sections, examples, blocks)
    over = [[s * n_dp + line * SIDE + x for s in sections for line in lines] for x in range(SIDE)]
    got = lax.all_to_all(send[:, None], BOTH, 0, 0, tiled=True, axis_index_groups=over)
    return total(got.reshape(send.shape))


def solution(mesh):
    placed = (
        P("section", "dp", None, None),
        P("section", "dp", None, None),
        P("section", None, None),
        P("section", "dp", None),
        P("dp"),
    )

    def body(*args):
        return on_device(mesh.shape["section"], mesh.shape["dp"], *args)

    return jax.shard_map(
        body, mesh=mesh, in_specs=placed, out_specs=P("dp", "section"), check_vma=False
    )
```

```python
import functools

import jax
import jax.numpy as jnp
from jax import lax
from jax.experimental import pallas as pl
from jax.experimental.pallas import tpu as pltpu
from jax.sharding import PartitionSpec as P

SIDE = 4
BOTH = ("section", "dp")
LANES = 128
ORDER = (2, 3, 1, 0)


def example_kernel(len_ref, in_ref, grad_ref, proj_ref, out_ref, staged):
    rank = proj_ref.shape[2] // 2
    table = proj_ref[0]
    input_side = jnp.dot(in_ref[0, 0], table, preferred_element_type=jnp.float32)
    grad_side = jnp.dot(grad_ref[0, 0], table, preferred_element_type=jnp.float32)
    input_side = input_side[:, :rank].astype(jnp.bfloat16)
    grad_side = grad_side[:, rank:].astype(jnp.bfloat16)
    count = len_ref[0]
    real = lax.broadcasted_iota(jnp.int32, grad_side.shape, 0) < count
    grad_side = jnp.where(real, grad_side, jnp.zeros_like(grad_side))
    summed = lax.dot_general(
        grad_side, input_side, (((0,), (0,)), ((), ())), preferred_element_type=jnp.float32
    )
    staged[...] = summed / count.astype(jnp.float32)
    half = rank // 2
    flat = jnp.concatenate(
        [staged[pl.ds(0, half, stride=2), :], staged[pl.ds(1, half, stride=2), :]], axis=1
    ).astype(jnp.bfloat16)
    for i in range(out_ref.shape[0]):
        out_ref[i] = flat


def example_copies(n_copies, lengths, layer_inputs, out_grads, projections):
    both = projections.shape[2]
    rank = both // 2
    vmem = pl.BlockSpec(memory_space=pltpu.VMEM)
    return pl.pallas_call(
        example_kernel,
        out_shape=jax.ShapeDtypeStruct((n_copies, rank * rank // LANES, LANES), jnp.bfloat16),
        in_specs=[pl.BlockSpec(memory_space=pltpu.SMEM), vmem, vmem, vmem],
        out_specs=vmem,
        scratch_shapes=[pltpu.VMEM((rank, rank), jnp.float32)],
        compiler_params=pltpu.CompilerParams(vmem_limit_bytes=16 << 20),
        cost_estimate=pl.CostEstimate(
            flops=COST_FLOPS, bytes_accessed=9 << 20, transcendentals=0
        ),
        name="example_gradient",
    )(lengths, layer_inputs, out_grads, projections)


COST_FLOPS = 1 << 31


def score_kernel(n_sections, got_ref, *rest):
    block_refs, (out_ref, wide) = rest[:SIDE], rest[SIDE:]
    index = lax.axis_index("dp")
    x_pos, z_pos = lax.rem(index, SIDE), lax.div(index, SIDE * SIDE)
    n, rows, lanes = got_ref.shape
    wide[...] = got_ref[...].reshape(n * rows, lanes).astype(jnp.float32)
    examples = jnp.concatenate(
        [wide[pl.ds(c, n, stride=rows), :] for c in range(rows)], axis=1
    ).astype(jnp.bfloat16)
    queries = jnp.concatenate([b[...] for b in block_refs], axis=0)
    scores = lax.dot_general(
        examples, queries, (((1,), (1,)), ((), ())), preferred_element_type=jnp.float32
    )
    width = scores.shape[1] // SIDE
    scores = pltpu.roll(scores, lax.div(x_pos, 2) * (2 * width), 1)
    lane = lax.broadcasted_iota(jnp.int32, scores.shape, 1)
    paired = jnp.where(
        lax.rem(lax.div(lane, width), 2) == 0,
        pltpu.roll(scores, (SIDE - 1) * width, 1),
        pltpu.roll(scores, width, 1),
    )
    scores = jnp.where(lax.rem(x_pos, 2) == 1, paired, scores)
    for s in range(n_sections):
        row = (n_sections - 1 - s) * n
        out_ref[row : row + n, :] = jnp.where(z_pos == s, scores, jnp.zeros_like(scores))


def score_rows(n_sections, examples, blocks):
    n, rows, lanes = examples.shape
    vmem = pl.BlockSpec(memory_space=pltpu.VMEM)
    return pl.pallas_call(
        functools.partial(score_kernel, n_sections),
        out_shape=jax.ShapeDtypeStruct((n_sections * n, SIDE * blocks[0].shape[0]), jnp.float32),
        in_specs=[vmem] * (1 + SIDE),
        out_specs=vmem,
        scratch_shapes=[pltpu.VMEM((n * rows, lanes), jnp.float32)],
        compiler_params=pltpu.CompilerParams(vmem_limit_bytes=8 << 20),
        name="scores",
    )(examples, *blocks)


def total_kernel(got_ref, out_ref):
    n, lanes = got_ref.shape
    lines = SIDE * SIDE
    summed = got_ref[0:lines, :]
    for r in range(lines, n, lines):
        summed = summed + got_ref[r : r + lines, :]
    for i, y in enumerate(ORDER):
        out_ref[:, y * lanes : (y + 1) * lanes] = jnp.sum(
            summed[i * SIDE : (i + 1) * SIDE], axis=0, keepdims=True
        )


def total(got):
    vmem = pl.BlockSpec(memory_space=pltpu.VMEM)
    return pl.pallas_call(
        total_kernel,
        out_shape=jax.ShapeDtypeStruct((1, SIDE * got.shape[1]), jnp.float32),
        in_specs=[vmem],
        out_specs=vmem,
        compiler_params=pltpu.CompilerParams(vmem_limit_bytes=4 << 20),
        name="total",
    )(got)


def keep_kernel(in_ref, out_ref):
    out_ref[...] = in_ref[0]


def kept(block):
    vmem = pl.BlockSpec(memory_space=pltpu.VMEM)
    return pl.pallas_call(
        keep_kernel,
        out_shape=jax.ShapeDtypeStruct(block.shape[1:], block.dtype),
        in_specs=[vmem],
        out_specs=vmem,
        compiler_params=pltpu.CompilerParams(vmem_limit_bytes=4 << 20),
        cost_estimate=pl.CostEstimate(flops=COST_FLOPS * 8, bytes_accessed=9 << 20, transcendentals=0),
        name="own_queries",
    )(block)


def on_device(n_sections, n_dp, layer_inputs, out_grads, projections, query_grads, lengths):
    n_lines = n_dp // SIDE

    own = kept(query_grads)
    blocks = [own]
    for k in range(1, SIDE):
        pairs = []
        for s in range(n_sections):
            for line in range(n_lines):
                base = s * n_dp + line * SIDE
                pairs += [(base + x, base + (x ^ k)) for x in range(SIDE)]
        blocks.append(lax.ppermute(own, BOTH, pairs))

    lines = [z * SIDE + y for y in ORDER for z in ORDER]
    sections = list(range(n_sections))[::-1]

    plane = [[line * SIDE + x for line in lines] for x in range(SIDE)]
    copies = example_copies(n_lines, lengths, layer_inputs, out_grads, projections)
    examples = lax.all_to_all(copies, "dp", 0, 0, tiled=True, axis_index_groups=plane)

    send = score_rows(n_sections, examples, blocks)
    over = [[s * n_dp + line * SIDE + x for s in sections for line in lines] for x in range(SIDE)]
    got = lax.all_to_all(send[:, None], BOTH, 0, 0, tiled=True, axis_index_groups=over)
    return total(got.reshape(send.shape))


def solution(mesh):
    placed = (
        P("section", "dp", None, None),
        P("section", "dp", None, None),
        P("section", None, None),
        P("section", "dp", None),
        P("dp"),
    )

    def body(*args):
        return on_device(mesh.shape["section"], mesh.shape["dp"], *args)

    return jax.shard_map(
        body, mesh=mesh, in_specs=placed, out_specs=P("dp", "section"), check_vma=False
    )
```

```python
import functools

import jax
import jax.numpy as jnp
from jax import lax
from jax.experimental import pallas as pl
from jax.experimental.pallas import tpu as pltpu
from jax.sharding import PartitionSpec as P

SIDE = 4
BOTH = ("section", "dp")
LANES = 128
ORDER = (2, 3, 1, 0)


def example_kernel(len_ref, in_ref, grad_ref, proj_ref, out_ref, staged):
    rank = proj_ref.shape[2] // 2
    table = proj_ref[0]
    input_side = jnp.dot(in_ref[0, 0], table, preferred_element_type=jnp.float32)
    grad_side = jnp.dot(grad_ref[0, 0], table, preferred_element_type=jnp.float32)
    input_side = input_side[:, :rank].astype(jnp.bfloat16)
    grad_side = grad_side[:, rank:].astype(jnp.bfloat16)
    count = len_ref[0]
    real = lax.broadcasted_iota(jnp.int32, grad_side.shape, 0) < count
    grad_side = jnp.where(real, grad_side, jnp.zeros_like(grad_side))
    summed = lax.dot_general(
        grad_side, input_side, (((0,), (0,)), ((), ())), preferred_element_type=jnp.float32
    )
    staged[...] = summed / count.astype(jnp.float32)
    half = rank // 2
    flat = jnp.concatenate(
        [staged[pl.ds(0, half, stride=2), :], staged[pl.ds(1, half, stride=2), :]], axis=1
    ).astype(jnp.bfloat16)
    for i in range(out_ref.shape[0]):
        out_ref[i] = flat


def example_copies(n_copies, lengths, layer_inputs, out_grads, projections):
    both = projections.shape[2]
    rank = both // 2
    vmem = pl.BlockSpec(memory_space=pltpu.VMEM)
    return pl.pallas_call(
        example_kernel,
        out_shape=jax.ShapeDtypeStruct((n_copies, rank * rank // LANES, LANES), jnp.bfloat16),
        in_specs=[pl.BlockSpec(memory_space=pltpu.SMEM), vmem, vmem, vmem],
        out_specs=vmem,
        scratch_shapes=[pltpu.VMEM((rank, rank), jnp.float32)],
        compiler_params=pltpu.CompilerParams(vmem_limit_bytes=16 << 20),
        cost_estimate=pl.CostEstimate(
            flops=COST_FLOPS, bytes_accessed=9 << 20, transcendentals=0
        ),
        name="example_gradient",
    )(lengths, layer_inputs, out_grads, projections)


COST_FLOPS = 1 << 31


def score_kernel(n_sections, got_ref, *rest):
    block_refs, (out_ref, wide) = rest[:SIDE], rest[SIDE:]
    index = lax.axis_index("dp")
    x_pos, z_pos = lax.rem(index, SIDE), lax.div(index, SIDE * SIDE)
    n, rows, lanes = got_ref.shape
    wide[...] = got_ref[...].reshape(n * rows, lanes).astype(jnp.float32)
    examples = jnp.concatenate(
        [wide[pl.ds(c, n, stride=rows), :] for c in range(rows)], axis=1
    ).astype(jnp.bfloat16)
    queries = jnp.concatenate([b[...] for b in block_refs], axis=0)
    scores = lax.dot_general(
        examples, queries, (((1,), (1,)), ((), ())), preferred_element_type=jnp.float32
    )
    width = scores.shape[1] // SIDE
    scores = pltpu.roll(scores, lax.div(x_pos, 2) * (2 * width), 1)
    lane = lax.broadcasted_iota(jnp.int32, scores.shape, 1)
    paired = jnp.where(
        lax.rem(lax.div(lane, width), 2) == 0,
        pltpu.roll(scores, (SIDE - 1) * width, 1),
        pltpu.roll(scores, width, 1),
    )
    scores = jnp.where(lax.rem(x_pos, 2) == 1, paired, scores)
    for s in range(n_sections):
        row = (n_sections - 1 - s) * n
        out_ref[row : row + n, :] = jnp.where(z_pos == s, scores, jnp.zeros_like(scores))


def score_rows(n_sections, examples, blocks):
    n, rows, lanes = examples.shape
    vmem = pl.BlockSpec(memory_space=pltpu.VMEM)
    return pl.pallas_call(
        functools.partial(score_kernel, n_sections),
        out_shape=jax.ShapeDtypeStruct((n_sections * n, SIDE * blocks[0].shape[0]), jnp.float32),
        in_specs=[vmem] * (1 + SIDE),
        out_specs=vmem,
        scratch_shapes=[pltpu.VMEM((n * rows, lanes), jnp.float32)],
        compiler_params=pltpu.CompilerParams(vmem_limit_bytes=8 << 20),
        name="scores",
    )(examples, *blocks)


def total_kernel(got_ref, marked_ref, out_ref):
    n, lanes = got_ref.shape
    lines = SIDE * SIDE
    summed = got_ref[0:lines, :]
    for r in range(lines, n, lines):
        summed = summed + got_ref[r : r + lines, :]
    for i, y in enumerate(ORDER):
        out_ref[:, y * lanes : (y + 1) * lanes] = jnp.sum(
            summed[i * SIDE : (i + 1) * SIDE], axis=0, keepdims=True
        )


def total(got, marked):
    vmem = pl.BlockSpec(memory_space=pltpu.VMEM)
    return pl.pallas_call(
        total_kernel,
        out_shape=jax.ShapeDtypeStruct((1, SIDE * got.shape[1]), jnp.float32),
        in_specs=[vmem, pl.BlockSpec(memory_space=pl.ANY)],
        out_specs=vmem,
        compiler_params=pltpu.CompilerParams(vmem_limit_bytes=4 << 20),
        name="total",
    )(got, marked)


def mark_kernel(out_ref):
    del out_ref


def mark():
    return pl.pallas_call(
        mark_kernel,
        out_shape=jax.ShapeDtypeStruct((8, LANES), jnp.int32),
        out_specs=pl.BlockSpec(memory_space=pl.ANY),
        compiler_params=pltpu.CompilerParams(vmem_limit_bytes=56064 << 10),
        cost_estimate=pl.CostEstimate(flops=7 << 30, bytes_accessed=1 << 10, transcendentals=0),
        name="mark",
    )()


def on_device(n_sections, n_dp, layer_inputs, out_grads, projections, query_grads, lengths):
    n_lines = n_dp // SIDE

    own, marked = lax.optimization_barrier((query_grads[0], mark()))
    blocks = [own]
    for k in range(1, SIDE):
        pairs = []
        for s in range(n_sections):
            for line in range(n_lines):
                base = s * n_dp + line * SIDE
                pairs += [(base + x, base + (x ^ k)) for x in range(SIDE)]
        blocks.append(lax.ppermute(own, BOTH, pairs))

    lines = [z * SIDE + y for y in ORDER for z in ORDER]
    sections = list(range(n_sections))[::-1]

    plane = [[line * SIDE + x for line in lines] for x in range(SIDE)]
    copies = example_copies(n_lines, lengths, layer_inputs, out_grads, projections)
    examples = lax.all_to_all(copies, "dp", 0, 0, tiled=True, axis_index_groups=plane)

    send = score_rows(n_sections, examples, blocks)
    over = [[s * n_dp + line * SIDE + x for s in sections for line in lines] for x in range(SIDE)]
    got = lax.all_to_all(send[:, None], BOTH, 0, 0, tiled=True, axis_index_groups=over)
    return total(got.reshape(send.shape), marked)


def solution(mesh):
    placed = (
        P("section", "dp", None, None),
        P("section", "dp", None, None),
        P("section", None, None),
        P("section", "dp", None),
        P("dp"),
    )

    def body(*args):
        return on_device(mesh.shape["section"], mesh.shape["dp"], *args)

    return jax.shard_map(
        body, mesh=mesh, in_specs=placed, out_specs=P("dp", "section"), check_vma=False
    )
```

```python
import functools

import jax
import jax.numpy as jnp
from jax import lax
from jax.experimental import pallas as pl
from jax.experimental.pallas import tpu as pltpu
from jax.sharding import PartitionSpec as P

SIDE = 4
BOTH = ("section", "dp")
LANES = 128
CHUNKS = 4
ORDER = (2, 3, 1, 0)


def example_kernel(len_ref, in_ref, grad_ref, proj_ref, out_ref, staged):
    model, both = proj_ref.shape[1:]
    rank, width = both // 2, model // CHUNKS
    input_side = grad_side = None
    for c in range(CHUNKS):
        cols = slice(c * width, (c + 1) * width)
        table = proj_ref[0, cols, :]
        a = jnp.dot(in_ref[0, 0, :, cols], table, preferred_element_type=jnp.float32)
        b = lax.dot_general(
            jnp.transpose(table)[rank:],
            grad_ref[0, 0, :, cols],
            (((1,), (1,)), ((), ())),
            preferred_element_type=jnp.float32,
        )
        input_side = a if input_side is None else input_side + a
        grad_side = b if grad_side is None else grad_side + b
    input_side = input_side[:, :rank].astype(jnp.bfloat16)
    grad_side = grad_side.astype(jnp.bfloat16)
    count = len_ref[0]
    real = lax.broadcasted_iota(jnp.int32, grad_side.shape, 1) < count
    grad_side = jnp.where(real, grad_side, jnp.zeros_like(grad_side))
    summed = jnp.dot(grad_side, input_side, preferred_element_type=jnp.float32)
    staged[...] = summed / count.astype(jnp.float32)
    half = rank // 2
    flat = jnp.concatenate(
        [staged[pl.ds(0, half, stride=2), :], staged[pl.ds(1, half, stride=2), :]], axis=1
    ).astype(jnp.bfloat16)
    for i in range(out_ref.shape[0]):
        out_ref[i] = flat


def example_copies(n_copies, lengths, layer_inputs, out_grads, projections):
    both = projections.shape[2]
    rank = both // 2
    vmem = pl.BlockSpec(memory_space=pltpu.VMEM)
    return pl.pallas_call(
        example_kernel,
        out_shape=jax.ShapeDtypeStruct((n_copies, rank * rank // LANES, LANES), jnp.bfloat16),
        in_specs=[pl.BlockSpec(memory_space=pltpu.SMEM), vmem, vmem, vmem],
        out_specs=vmem,
        scratch_shapes=[pltpu.VMEM((rank, rank), jnp.float32)],
        compiler_params=pltpu.CompilerParams(vmem_limit_bytes=16 << 20),
        cost_estimate=pl.CostEstimate(
            flops=COST_FLOPS, bytes_accessed=9 << 20, transcendentals=0
        ),
        name="example_gradient",
    )(lengths, layer_inputs, out_grads, projections)


COST_FLOPS = 1 << 31


def score_kernel(n_sections, got_ref, *rest):
    block_refs, (out_ref, wide) = rest[:SIDE], rest[SIDE:]
    index = lax.axis_index("dp")
    x_pos, z_pos = lax.rem(index, SIDE), lax.div(index, SIDE * SIDE)
    n, rows, lanes = got_ref.shape
    wide[...] = got_ref[...].reshape(n * rows, lanes).astype(jnp.float32)
    examples = jnp.concatenate(
        [wide[pl.ds(c, n, stride=rows), :] for c in range(rows)], axis=1
    ).astype(jnp.bfloat16)
    queries = jnp.concatenate([b[...] for b in block_refs], axis=0)
    scores = lax.dot_general(
        examples, queries, (((1,), (1,)), ((), ())), preferred_element_type=jnp.float32
    )
    width = scores.shape[1] // SIDE
    scores = pltpu.roll(scores, lax.div(x_pos, 2) * (2 * width), 1)
    lane = lax.broadcasted_iota(jnp.int32, scores.shape, 1)
    paired = jnp.where(
        lax.rem(lax.div(lane, width), 2) == 0,
        pltpu.roll(scores, (SIDE - 1) * width, 1),
        pltpu.roll(scores, width, 1),
    )
    scores = jnp.where(lax.rem(x_pos, 2) == 1, paired, scores)
    for s in range(n_sections):
        row = (n_sections - 1 - s) * n
        out_ref[row : row + n, :] = jnp.where(z_pos == s, scores, jnp.zeros_like(scores))


def score_rows(n_sections, examples, blocks):
    n, rows, lanes = examples.shape
    vmem = pl.BlockSpec(memory_space=pltpu.VMEM)
    return pl.pallas_call(
        functools.partial(score_kernel, n_sections),
        out_shape=jax.ShapeDtypeStruct((n_sections * n, SIDE * blocks[0].shape[0]), jnp.float32),
        in_specs=[vmem] * (1 + SIDE),
        out_specs=vmem,
        scratch_shapes=[pltpu.VMEM((n * rows, lanes), jnp.float32)],
        compiler_params=pltpu.CompilerParams(vmem_limit_bytes=8 << 20),
        name="scores",
    )(examples, *blocks)


def total_kernel(got_ref, marked_ref, out_ref):
    n, lanes = got_ref.shape
    lines = SIDE * SIDE
    summed = got_ref[0:lines, :]
    for r in range(lines, n, lines):
        summed = summed + got_ref[r : r + lines, :]
    for i, y in enumerate(ORDER):
        out_ref[:, y * lanes : (y + 1) * lanes] = jnp.sum(
            summed[i * SIDE : (i + 1) * SIDE], axis=0, keepdims=True
        )


def total(got, marked):
    vmem = pl.BlockSpec(memory_space=pltpu.VMEM)
    return pl.pallas_call(
        total_kernel,
        out_shape=jax.ShapeDtypeStruct((1, SIDE * got.shape[1]), jnp.float32),
        in_specs=[vmem, pl.BlockSpec(memory_space=pl.ANY)],
        out_specs=vmem,
        compiler_params=pltpu.CompilerParams(vmem_limit_bytes=4 << 20),
        name="total",
    )(got, marked)


def mark_kernel(out_ref):
    del out_ref


def mark():
    return pl.pallas_call(
        mark_kernel,
        out_shape=jax.ShapeDtypeStruct((8, LANES), jnp.int32),
        out_specs=pl.BlockSpec(memory_space=pl.ANY),
        compiler_params=pltpu.CompilerParams(vmem_limit_bytes=56064 << 10),
        cost_estimate=pl.CostEstimate(flops=7 << 30, bytes_accessed=1 << 10, transcendentals=0),
        name="mark",
    )()


def on_device(n_sections, n_dp, layer_inputs, out_grads, projections, query_grads, lengths):
    n_lines = n_dp // SIDE

    own, marked = lax.optimization_barrier((query_grads[0], mark()))
    blocks = [own]
    for k in range(1, SIDE):
        pairs = []
        for s in range(n_sections):
            for line in range(n_lines):
                base = s * n_dp + line * SIDE
                pairs += [(base + x, base + (x ^ k)) for x in range(SIDE)]
        blocks.append(lax.ppermute(own, BOTH, pairs))

    lines = [z * SIDE + y for y in ORDER for z in ORDER]
    sections = list(range(n_sections))[::-1]

    plane = [[line * SIDE + x for line in lines] for x in range(SIDE)]
    copies = example_copies(n_lines, lengths, layer_inputs, out_grads, projections)
    examples = lax.all_to_all(copies, "dp", 0, 0, tiled=True, axis_index_groups=plane)

    send = score_rows(n_sections, examples, blocks)
    over = [[s * n_dp + line * SIDE + x for s in sections for line in lines] for x in range(SIDE)]
    got = lax.all_to_all(send[:, None], BOTH, 0, 0, tiled=True, axis_index_groups=over)
    return total(got.reshape(send.shape), marked)


def solution(mesh):
    placed = (
        P("section", "dp", None, None),
        P("section", "dp", None, None),
        P("section", None, None),
        P("section", "dp", None),
        P("dp"),
    )

    def body(*args):
        return on_device(mesh.shape["section"], mesh.shape["dp"], *args)

    return jax.shard_map(
        body, mesh=mesh, in_specs=placed, out_specs=P("dp", "section"), check_vma=False
    )
```

```python
import functools

import jax
import jax.numpy as jnp
from jax import lax
from jax.experimental import pallas as pl
from jax.experimental.pallas import tpu as pltpu
from jax.sharding import PartitionSpec as P

SIDE = 4
BOTH = ("section", "dp")
LANES = 128
CHUNKS = 4
ORDER = (2, 3, 1, 0)


def section_order(n_sections):
    return sorted(range(n_sections), key=lambda s: (-(s % 2), -s))


def example_kernel(len_ref, in_ref, grad_ref, proj_ref, out_ref, staged):
    model, both = proj_ref.shape[1:]
    rank, width = both // 2, model // CHUNKS
    input_side = grad_side = None
    for c in range(CHUNKS):
        cols = slice(c * width, (c + 1) * width)
        table = proj_ref[0, cols, :]
        a = jnp.dot(in_ref[0, 0, :, cols], table, preferred_element_type=jnp.float32)
        b = lax.dot_general(
            jnp.transpose(table)[rank:],
            grad_ref[0, 0, :, cols],
            (((1,), (1,)), ((), ())),
            preferred_element_type=jnp.float32,
        )
        input_side = a if input_side is None else input_side + a
        grad_side = b if grad_side is None else grad_side + b
    input_side = input_side[:, :rank].astype(jnp.bfloat16)
    grad_side = grad_side.astype(jnp.bfloat16)
    count = len_ref[0]
    real = lax.broadcasted_iota(jnp.int32, grad_side.shape, 1) < count
    grad_side = jnp.where(real, grad_side, jnp.zeros_like(grad_side))
    summed = jnp.dot(grad_side, input_side, preferred_element_type=jnp.float32)
    staged[...] = summed / count.astype(jnp.float32)
    half = rank // 2
    flat = jnp.concatenate(
        [staged[pl.ds(0, half, stride=2), :], staged[pl.ds(1, half, stride=2), :]], axis=1
    ).astype(jnp.bfloat16)
    for i in range(out_ref.shape[0]):
        out_ref[i] = flat


def example_copies(n_copies, lengths, layer_inputs, out_grads, projections):
    both = projections.shape[2]
    rank = both // 2
    vmem = pl.BlockSpec(memory_space=pltpu.VMEM)
    return pl.pallas_call(
        example_kernel,
        out_shape=jax.ShapeDtypeStruct((n_copies, rank * rank // LANES, LANES), jnp.bfloat16),
        in_specs=[pl.BlockSpec(memory_space=pltpu.SMEM), vmem, vmem, vmem],
        out_specs=vmem,
        scratch_shapes=[pltpu.VMEM((rank, rank), jnp.float32)],
        compiler_params=pltpu.CompilerParams(vmem_limit_bytes=16 << 20),
        cost_estimate=pl.CostEstimate(
            flops=COST_FLOPS, bytes_accessed=9 << 20, transcendentals=0
        ),
        name="example_gradient",
    )(lengths, layer_inputs, out_grads, projections)


COST_FLOPS = 1 << 31


def score_kernel(n_sections, got_ref, *rest):
    block_refs, (out_ref, wide) = rest[:SIDE], rest[SIDE:]
    index = lax.axis_index("dp")
    x_pos, z_pos = lax.rem(index, SIDE), lax.div(index, SIDE * SIDE)
    n, rows, lanes = got_ref.shape
    wide[...] = got_ref[...].reshape(n * rows, lanes).astype(jnp.float32)
    examples = jnp.concatenate(
        [wide[pl.ds(c, n, stride=rows), :] for c in range(rows)], axis=1
    ).astype(jnp.bfloat16)
    queries = jnp.concatenate([b[...] for b in block_refs], axis=0)
    scores = lax.dot_general(
        examples, queries, (((1,), (1,)), ((), ())), preferred_element_type=jnp.float32
    )
    width = scores.shape[1] // SIDE
    scores = pltpu.roll(scores, lax.div(x_pos, 2) * (2 * width), 1)
    lane = lax.broadcasted_iota(jnp.int32, scores.shape, 1)
    paired = jnp.where(
        lax.rem(lax.div(lane, width), 2) == 0,
        pltpu.roll(scores, (SIDE - 1) * width, 1),
        pltpu.roll(scores, width, 1),
    )
    scores = jnp.where(lax.rem(x_pos, 2) == 1, paired, scores)
    for s in range(n_sections):
        row = section_order(n_sections).index(s) * n
        out_ref[row : row + n, :] = jnp.where(z_pos == s, scores, jnp.zeros_like(scores))


def score_rows(n_sections, examples, blocks):
    n, rows, lanes = examples.shape
    vmem = pl.BlockSpec(memory_space=pltpu.VMEM)
    return pl.pallas_call(
        functools.partial(score_kernel, n_sections),
        out_shape=jax.ShapeDtypeStruct((n_sections * n, SIDE * blocks[0].shape[0]), jnp.float32),
        in_specs=[vmem] * (1 + SIDE),
        out_specs=vmem,
        scratch_shapes=[pltpu.VMEM((n * rows, lanes), jnp.float32)],
        compiler_params=pltpu.CompilerParams(vmem_limit_bytes=8 << 20),
        name="scores",
    )(examples, *blocks)


def total_kernel(got_ref, marked_ref, out_ref):
    n, lanes = got_ref.shape
    lines = SIDE * SIDE
    summed = got_ref[0:lines, :]
    for r in range(lines, n, lines):
        summed = summed + got_ref[r : r + lines, :]
    for i, y in enumerate(ORDER):
        out_ref[:, y * lanes : (y + 1) * lanes] = jnp.sum(
            summed[i * SIDE : (i + 1) * SIDE], axis=0, keepdims=True
        )


def total(got, marked):
    vmem = pl.BlockSpec(memory_space=pltpu.VMEM)
    return pl.pallas_call(
        total_kernel,
        out_shape=jax.ShapeDtypeStruct((1, SIDE * got.shape[1]), jnp.float32),
        in_specs=[vmem, pl.BlockSpec(memory_space=pl.ANY)],
        out_specs=vmem,
        compiler_params=pltpu.CompilerParams(vmem_limit_bytes=4 << 20),
        name="total",
    )(got, marked)


def mark_kernel(out_ref):
    del out_ref


def mark():
    return pl.pallas_call(
        mark_kernel,
        out_shape=jax.ShapeDtypeStruct((8, LANES), jnp.int32),
        out_specs=pl.BlockSpec(memory_space=pl.ANY),
        compiler_params=pltpu.CompilerParams(vmem_limit_bytes=56064 << 10),
        cost_estimate=pl.CostEstimate(flops=7 << 30, bytes_accessed=1 << 10, transcendentals=0),
        name="mark",
    )()


def on_device(n_sections, n_dp, layer_inputs, out_grads, projections, query_grads, lengths):
    n_lines = n_dp // SIDE

    own, marked = lax.optimization_barrier((query_grads[0], mark()))
    blocks = [own]
    for k in range(1, SIDE):
        pairs = []
        for s in range(n_sections):
            for line in range(n_lines):
                base = s * n_dp + line * SIDE
                pairs += [(base + x, base + (x ^ k)) for x in range(SIDE)]
        blocks.append(lax.ppermute(own, BOTH, pairs))

    lines = [z * SIDE + y for y in ORDER for z in ORDER]
    sections = section_order(n_sections)

    plane = [[line * SIDE + x for line in lines] for x in range(SIDE)]
    copies = example_copies(n_lines, lengths, layer_inputs, out_grads, projections)
    examples = lax.all_to_all(copies, "dp", 0, 0, tiled=True, axis_index_groups=plane)

    send = score_rows(n_sections, examples, blocks)
    over = [[s * n_dp + line * SIDE + x for s in sections for line in lines] for x in range(SIDE)]
    got = lax.all_to_all(send[:, None], BOTH, 0, 0, tiled=True, axis_index_groups=over)
    return total(got.reshape(send.shape), marked)


def solution(mesh):
    placed = (
        P("section", "dp", None, None),
        P("section", "dp", None, None),
        P("section", None, None),
        P("section", "dp", None),
        P("dp"),
    )

    def body(*args):
        return on_device(mesh.shape["section"], mesh.shape["dp"], *args)

    return jax.shard_map(
        body, mesh=mesh, in_specs=placed, out_specs=P("dp", "section"), check_vma=False
    )
```
